32 devices in a mesh: ens: 4 (over y, core), space: 8 (over z, x).
Axes of the slice: x: 2, y: 2, z: 4, core: 2. Of those that a mesh axis runs over, the one named last changes fastest.
Arguments:
- prior_profiles: bfloat16 [128, 64, 64, 128], P('ens', 'space'), may hold values from -6 to 6
- conductivity_profile: bfloat16 [128, 64, 64, 128], P('ens', 'space'), may hold values from 0.5 to 2
- sensor_position_flat: int32 [8192], P('space'), may hold values from 0 to 65535
- observation_slot_count: int32 [8], P('space'), may hold values from 1 to 1024, 5120 in all
- obs_values: float32 [8192], P('space'), may hold values from -6 to 6
- obs_std: float32 [8192], P('space'), may hold values from 0.3 to 3
- obs_noise: float32 [128, 8192], P('ens', 'space'), may hold values from -6 to 6
- params: float32 [128, 2048], P('ens', 'space'), may hold values from -6 to 6
Outputs:
- posterior_parameters: float32 [128, 2048], P('ens', 'space')
- predicted_states: float32 [128, 64, 64, 128], P('ens', 'space')
The draws below stay inside these ranges and needn't reach their ends.
Inputs may be any that keep to these rules, and one draw needn't show every extreme that they name: The live slots of a slab are its first observation_slot_count ones.
All inputs are finite; a program needn't handle non-finite values. No bound on the sum of `observation_slot_count` on one device may be relied on, other than what follows from the above.
Results may differ from the reference program's by a relative error of at most 0.0003.
Values may be sent and summed in bfloat16 or wider, within the bound.
A program may use at most 256 MiB of HBM per device.

```python
import math
import jax
import jax.numpy as jnp
import numpy as np
from jax import lax

M = 128
CZ = 8
NX = 64
NY = 128
NZ = 64
P_SIZE = 2048
OBS_CAP = 1024
OBS = 8192
N_SPACE = 8


def touch_ends(values, key, least, largest):
    spot = [jax.random.randint(jax.random.fold_in(key, axis), (), 0, length) for axis, length in enumerate(values.shape)]
    widest = values.shape.index(max(values.shape))
    beside = spot[:widest] + [(spot[widest] + 1) % values.shape[widest]] + spot[widest + 1:]
    return values.at[tuple(spot)].set(least).at[tuple(beside)].set(largest)


def block_scale(stream_key, shape, cuts, smallest, top_value):
    level = 1.0
    for dim, shards_of in cuts:
        heights = jax.random.uniform(jax.random.fold_in(jax.random.fold_in(stream_key, 6), dim), (shards_of,), jnp.float32, smallest / len(cuts), top_value / len(cuts))
        level = level * jnp.repeat(jnp.exp(heights), shape[dim] // shards_of).reshape((-1,) + (1,) * (len(shape) - 1 - dim))
    return level


def profile(amount, total, limit, lean):
    weights = [(1 << 20) // math.isqrt(standing ** lean) + 1 for standing in range(2, amount + 1)]
    surplus, given = total - limit - (amount - 1), [1] * (amount - 1)
    while surplus > 0:
        movable = [i for i in range(amount - 1) if given[i] < limit]
        mass, left = sum([weights[i] for i in movable]), surplus
        for i in movable:
            addition = min(limit - given[i], max(1, left * weights[i] // mass), surplus)
            given[i] = given[i] + addition
            surplus = surplus - addition
    return np.array([limit] + given)


def ragged(own_key, amount, total, most, slope):
    if amount == 2:
        one = jax.random.randint(own_key, (), max(1, total - most), min(most, total - 1) + 1)
        return jnp.stack([one, total - one])
    sizes = jnp.asarray(profile(amount, total, most, slope), jnp.int32)
    twos = (amount - 1) // 2
    source_of, receiver = sizes[1:1 + 2 * twos:2], sizes[2:2 + 2 * twos:2]
    slack = jnp.minimum(source_of - 1, most - receiver)
    passed = jax.random.randint(jax.random.fold_in(own_key, 1), (twos,), 0, 1 << 20) % (slack + 1)
    sizes = sizes.at[1:1 + 2 * twos:2].set(source_of - passed).at[2:2 + 2 * twos:2].set(receiver + passed)
    return sizes[jax.random.permutation(jax.random.fold_in(own_key, 2), amount)]


def centred(stream_key, shape, width, limit, shards=(), held_as=jnp.bfloat16):
    values = width * jax.random.normal(stream_key, shape, jnp.float32)
    if shards:
        values = values * block_scale(stream_key, shape, shards, -0.22, 0.18)
    return jnp.clip(values, -limit, limit).astype(held_as)


def setup_inputs(seed: int = 0) -> dict:
    seeds = jax.random.split(jax.random.key(seed), 9)
    return {
        "prior_profiles": centred(seeds[0], (M, NZ, NX, NY), 1.0, 6.0, ((0, 4), (1, 8))),
        "conductivity_profile": jnp.clip(jnp.exp(math.log(2.0) - 1.3862944 * jax.random.uniform(seeds[1], (M, NZ, NX, NY), jnp.float32) ** block_scale(seeds[1], (M, NZ, NX, NY), ((0, 4), (1, 8)), -0.2, 0.2)), 0.5, 2.0).astype(jnp.bfloat16),
        "sensor_position_flat": touch_ends(jax.random.randint(seeds[2], (OBS,), 0, CZ * NX * NY), jax.random.fold_in(seeds[2], 1), 0, (CZ * NX * NY) - 1).astype(jnp.int32),
        "observation_slot_count": ragged(seeds[3], N_SPACE, N_SPACE * OBS_CAP * 5 // 8, OBS_CAP, 2).astype(jnp.int32),
        "obs_values": centred(seeds[4], (OBS,), 1.0, 6.0, ((0, 8),), jnp.float32),
        "obs_std": jnp.clip(jnp.exp(math.log(3.0) - 2.3025851 * jax.random.uniform(seeds[5], (OBS,), jnp.float32) ** block_scale(seeds[5], (OBS,), ((0, 8),), -0.2, 0.2)), 0.3, 3.0),
        "obs_noise": centred(seeds[6], (M, OBS), 1.0, 6.0, ((0, 4), (1, 8)), jnp.float32),
        "params": centred(seeds[7], (M, P_SIZE), 1.0, 6.0, ((0, 4), (1, 8)), jnp.float32),
    }


step_size = 0.08

def inner_window(array, starts):
    for dimension in range(3):
        which_axis = array.ndim - 3 + dimension
        extent = array.shape[which_axis] - 2
        array = lax.slice_in_dim(array, starts[dimension], starts[dimension] + extent, axis=which_axis)
    return array

def spread_heat_onestep(field, coeff):
    centre_u = inner_window(field, (1, 1, 1))
    centre_k = inner_window(coeff, (1, 1, 1))
    flux = jnp.zeros_like(centre_u)
    for dimension in range(3):
        for offset in (0, 2):
            starts = [1, 1, 1]
            starts[dimension] = offset
            neigh_u = inner_window(field, tuple(starts))
            neigh_k = inner_window(coeff, tuple(starts))
            flux = flux + 0.5 * (centre_k + neigh_k) * (neigh_u - centre_u)
    return centre_u + step_size * flux

def reference(prior_profiles, conductivity_profile, sensor_position_flat, observation_slot_count, obs_values, obs_std, obs_noise, params):
    cell_table = sensor_position_flat.reshape(N_SPACE, OBS_CAP)

    def realization_march(pair):
        field = jnp.pad(pair[0].astype(jnp.float32), 1)
        coeff = jnp.pad(pair[1].astype(jnp.float32), 1)
        result = spread_heat_onestep(field, coeff)
        slabs = result.reshape(N_SPACE, CZ * NX * NY)
        selected_members = jnp.take_along_axis(slabs, cell_table, axis=1).reshape(OBS)
        return (result, selected_members)
    predicted_states, sampled_readings = lax.map(realization_march, (prior_profiles, conductivity_profile))
    slot_index = jnp.arange(OBS, dtype=jnp.int32) % OBS_CAP
    live_slots = slot_index < jnp.repeat(observation_slot_count, OBS_CAP)
    ens_scale = math.sqrt(M - 1.0)
    centre = lax.optimization_barrier(jnp.mean(sampled_readings, axis=0))
    spread = jnp.where(live_slots, (sampled_readings - centre) / (obs_std * ens_scale), 0.0)
    misfit = jnp.where(live_slots, (obs_values - sampled_readings) / obs_std + obs_noise, 0.0)
    gram_matrix = jnp.dot(spread, spread.T, precision=lax.Precision.HIGHEST)
    cross_term = jnp.dot(spread, misfit.T, precision=lax.Precision.HIGHEST)
    factor = jnp.linalg.cholesky(gram_matrix + jnp.eye(M, dtype=jnp.float32))
    weights = jax.scipy.linalg.cho_solve((factor, True), cross_term)
    anomaly = (params - lax.optimization_barrier(jnp.mean(params, axis=0))) / ens_scale
    posterior_parameters = params + jnp.dot(weights.T, anomaly, precision=lax.Precision.HIGHEST)
    return (posterior_parameters, predicted_states)
```

```python
import functools
import math

import jax
import jax.numpy as jnp
from jax import lax
from jax.experimental import pallas as pl
from jax.experimental.pallas import tpu as pltpu
from jax.sharding import PartitionSpec as P

half_step = 0.04
HI = lax.Precision.HIGHEST
MESH = pl.DeviceIdType.MESH


def stencil_kernel(u_ref, k_ref, o_ref):
    members, cz, nx, ny = u_ref.shape
    row = lax.broadcasted_iota(jnp.int32, (nx, ny), 0)
    lane = lax.broadcasted_iota(jnp.int32, (nx, ny), 1)
    first_x, last_x = row == 0, row == nx - 1
    first_y, last_y = lane == 0, lane == ny - 1

    def member(m, carry):
        below = None
        u = u_ref[m, 0].astype(jnp.float32)
        k = k_ref[m, 0].astype(jnp.float32)
        for z in range(cz):
            ku = k * u
            fx = (k + pltpu.roll(k, nx - 1, 0)) * (pltpu.roll(u, nx - 1, 0) - u)
            total = jnp.where(last_x, -ku, fx) - jnp.where(first_x, ku, pltpu.roll(fx, 1, 0))
            fy = (k + pltpu.roll(k, ny - 1, 1)) * (pltpu.roll(u, ny - 1, 1) - u)
            total += jnp.where(last_y, -ku, fy) - jnp.where(first_y, ku, pltpu.roll(fy, 1, 1))
            if below is not None:
                total -= below
            if z < cz - 1:
                u_next = u_ref[m, z + 1].astype(jnp.float32)
                k_next = k_ref[m, z + 1].astype(jnp.float32)
                below = (k + k_next) * (u_next - u)
                total += below
            o_ref[m, z] = u + half_step * total
            if z < cz - 1:
                u, k = u_next, k_next
        return carry

    lax.fori_loop(0, members, member, 0)


def stencil(u, k):
    m, cz, nx, ny = u.shape
    block = 4
    spec = pl.BlockSpec((block, cz, nx, ny), lambda g: (g, 0, 0, 0))
    return pl.pallas_call(
        stencil_kernel,
        grid=(m // block,),
        in_specs=[spec, spec],
        out_specs=spec,
        out_shape=jax.ShapeDtypeStruct(u.shape, jnp.float32),
        cost_estimate=pl.CostEstimate(
            flops=40 * u.size, bytes_accessed=8 * u.size, transcendentals=0
        ),
        name="stencil",
    )(u, k)


def border_kernel(
    row_ref, col_ref, p_ref, u_ref, k_ref, ulo_ref, klo_ref, uhi_ref, khi_ref,
    o_ref, picked_ref, scr,
):
    g, e = pl.program_id(0), pl.program_id(1)
    block, cz, nx, ny = p_ref.shape
    cells = cz * nx
    members = scr.shape[0] // cells
    base = g * block
    u = u_ref[:, 0].astype(jnp.float32)
    k = k_ref[:, 0].astype(jnp.float32)

    def fix(z, un_ref, kn_ref):
        un = un_ref[...].astype(jnp.float32)
        kn = kn_ref[...].astype(jnp.float32)
        new = p_ref[:, z] + half_step * (k + kn) * (un - u)
        o_ref[:, 0] = new
        for b in range(block):
            start = pl.multiple_of((base + b) * cells + z * nx, nx)
            scr[pl.ds(start, nx), :] = new[b]

    @pl.when(e == 0)
    def _():
        fix(0, ulo_ref, klo_ref)
        for b in range(block):
            for z in range(1, cz - 1):
                start = pl.multiple_of((base + b) * cells + z * nx, nx)
                scr[pl.ds(start, nx), :] = p_ref[b, z]

    @pl.when(e == 1)
    def _():
        fix(cz - 1, uhi_ref, khi_ref)

    @pl.when(jnp.logical_and(g == pl.num_programs(0) - 1, e == 1))
    def _():
        lane = lax.broadcasted_iota(jnp.int32, (8, ny), 1)
        groups = members // 8
        unroll = 8

        def chunk(c, carry):
            def step(s, acc):
                acc = list(acc)
                for i in range(unroll):
                    jj = s * unroll + i
                    j = c * ny + jj
                    r, shift = row_ref[j], col_ref[j]
                    here = lane == jj
                    for q in range(groups):
                        v = scr[pl.ds(r + q * 8 * cells, 8, stride=cells), :]
                        acc[q] = jnp.where(here, pltpu.roll(v, shift, 1), acc[q])
                return tuple(acc)

            zero = jnp.zeros((8, ny), jnp.float32)
            acc = lax.fori_loop(0, ny // unroll, step, (zero,) * groups)
            for q in range(groups):
                picked_ref[q * 8 : (q + 1) * 8, pl.ds(pl.multiple_of(c * ny, ny), ny)] = acc[q]
            return carry

        lax.fori_loop(0, picked_ref.shape[1] // ny, chunk, 0)


def border(pred, u, k, ulo, klo, uhi, khi, position):
    m, cz, nx, ny = u.shape
    slots = position.shape[0]
    block = 8
    row = position // ny
    slot = jnp.arange(slots, dtype=jnp.int32)
    shift = (slot - position % ny) % ny
    edge = pl.BlockSpec((block, 1, nx, ny), lambda g, e, *_: (g, e * (cz - 1), 0, 0))
    halo = pl.BlockSpec((block, nx, ny), lambda g, e, *_: (g, 0, 0))
    return pl.pallas_call(
        border_kernel,
        grid_spec=pltpu.PrefetchScalarGridSpec(
            num_scalar_prefetch=2,
            grid=(m // block, 2),
            in_specs=[
                pl.BlockSpec((block, cz, nx, ny), lambda g, e, *_: (g, 0, 0, 0)),
                edge, edge, halo, halo, halo, halo,
            ],
            out_specs=[edge, pl.BlockSpec((m, slots), lambda g, e, *_: (0, 0))],
            scratch_shapes=[pltpu.VMEM((m * cz * nx, ny), jnp.float32)],
        ),
        out_shape=[
            jax.ShapeDtypeStruct(u.shape, jnp.float32),
            jax.ShapeDtypeStruct((m, slots), jnp.float32),
        ],
        input_output_aliases={2: 0},
        name="border",
    )(row, shift, pred, u, k, ulo, klo, uhi, khi)


def products_kernel(
    n_e, n_s, count_ref, picked_ref, noise_ref, values_ref, std_ref, params_ref,
    gram_ref, cross_ref, all_params_ref,
    all_picked, part, parts, total,
    send_a, recv_a, send_p, recv_p, send_s, recv_s, send_g, recv_g,
):
    own, slots = picked_ref.shape
    members = own * n_e
    me_e, me_s = lax.axis_index("ens"), lax.axis_index("space")
    scale = math.sqrt(members - 1.0)

    def ens_peer(d):
        return (lax.rem(me_e + d, n_e), me_s)

    def space_peer(d):
        return (me_e, lax.rem(me_s + d, n_s))

    barrier = pltpu.get_barrier_semaphore()
    for d in range(1, n_e):
        pl.semaphore_signal(barrier, inc=1, device_id=ens_peer(d), device_id_type=MESH)
    for d in range(1, n_s):
        pl.semaphore_signal(barrier, inc=1, device_id=space_peer(d), device_id_type=MESH)
    pl.semaphore_wait(barrier, n_e + n_s - 2)

    def send(src, dst, ssem, rsem, peer):
        copy = pltpu.make_async_remote_copy(
            src_ref=src, dst_ref=dst, send_sem=ssem, recv_sem=rsem,
            device_id=peer, device_id_type=MESH,
        )
        copy.start()
        return copy

    picked_copies = [
        send(picked_ref, all_picked.at[me_e], send_a.at[d], recv_a.at[d], ens_peer(d))
        for d in range(1, n_e)
    ]
    params_copies = [
        send(params_ref, all_params_ref.at[me_e], send_p.at[d], recv_p.at[d], ens_peer(d))
        for d in range(1, n_e)
    ]
    all_params_ref[me_e] = params_ref[...]
    mine = picked_ref[...]
    all_picked[me_e] = mine
    live = lax.broadcasted_iota(jnp.int32, (1, slots), 1) < count_ref[0]
    std = std_ref[...]
    inverse = jnp.where(live, 1.0 / (std * scale), 0.0)
    misfit = jnp.where(live, (values_ref[...] - mine) / std + noise_ref[...], 0.0)
    for copy in picked_copies:
        copy.wait()
    everyone = all_picked[...].reshape(members, slots)
    centre = jnp.sum(everyone, axis=0, keepdims=True) / members
    spread = (everyone - centre) * inverse
    left = jnp.concatenate([(mine - centre) * inverse, misfit], axis=0)
    part[...] = lax.dot_general(
        left, spread, (((1,), (1,)), ((), ())),
        precision=HI, preferred_element_type=jnp.float32,
    )
    space_copies = [
        send(part, parts.at[d], send_s.at[d], recv_s.at[d], space_peer(d)) for d in range(1, n_s)
    ]
    acc = part[...]
    for d in range(1, n_s):
        space_copies[d - 1].wait()
        acc += parts[d]
    total[...] = acc[:own]
    gram_copies = [
        send(total, gram_ref.at[me_e], send_g.at[d], recv_g.at[d], ens_peer(d))
        for d in range(1, n_e)
    ]
    gram_ref[me_e] = acc[:own]
    cross_ref[...] = acc[own:]
    for copy in gram_copies:
        copy.wait()
    for copy in params_copies:
        copy.wait()


def products(n_e, n_s, count, picked, noise, values, std, params):
    own, slots = picked.shape
    vmem = pl.BlockSpec(memory_space=pltpu.VMEM)
    dma = pltpu.SemaphoreType.DMA
    return pl.pallas_call(
        functools.partial(products_kernel, n_e, n_s),
        in_specs=[pl.BlockSpec(memory_space=pltpu.SMEM)] + [vmem] * 5,
        out_specs=[vmem] * 3,
        out_shape=[
            jax.ShapeDtypeStruct((n_e, own, n_e * own), jnp.float32),
            jax.ShapeDtypeStruct((own, n_e * own), jnp.float32),
            jax.ShapeDtypeStruct((n_e,) + params.shape, jnp.float32),
        ],
        scratch_shapes=[
            pltpu.VMEM((n_e, own, slots), jnp.float32),
            pltpu.VMEM((2 * own, n_e * own), jnp.float32),
            pltpu.VMEM((n_s, 2 * own, n_e * own), jnp.float32),
            pltpu.VMEM((own, n_e * own), jnp.float32),
        ]
        + [dma((n_e,))] * 4 + [dma((n_s,))] * 2 + [dma((n_e,))] * 2,
        compiler_params=pltpu.CompilerParams(collective_id=0, has_side_effects=True),
        name="products",
    )(count, picked, noise, values.reshape(1, -1), std.reshape(1, -1), params)


def update_kernel(gram_ref, cross_ref, all_params_ref, params_ref, o_ref, work):
    members = gram_ref.shape[1]
    own = cross_ref.shape[0]
    rows = lax.broadcasted_iota(jnp.int32, (members, members), 0)
    cols = lax.broadcasted_iota(jnp.int32, (members, members), 1)
    lane = lax.broadcasted_iota(jnp.int32, (1, members), 1)
    work[:members] = gram_ref[...] + jnp.where(rows == cols, 1.0, 0.0)
    work[members:] = cross_ref[...]

    def step(k, diagonal):
        here = lane == k
        row = work[pl.ds(k, 1), :]
        pivot = jnp.sum(jnp.where(here, row, 0.0), axis=1, keepdims=True)
        factor = jnp.where(here, 0.0, row / pivot)
        t = work[...]
        column = jnp.sum(jnp.where(here, t, 0.0), axis=1, keepdims=True)
        work[...] = t - column * factor
        return jnp.where(here, pivot, diagonal)

    diagonal = lax.fori_loop(0, members, step, jnp.ones((1, members), jnp.float32))
    weights = work[members:] / diagonal
    all_params = all_params_ref[...]
    centre = jnp.sum(all_params, axis=0, keepdims=True) / members
    anomaly = (all_params - centre) / math.sqrt(members - 1.0)
    o_ref[...] = params_ref[...] + jnp.dot(
        weights, anomaly, precision=HI, preferred_element_type=jnp.float32
    )


def update(gram, cross, all_params, params):
    members, own = gram.shape[2], cross.shape[0]
    return pl.pallas_call(
        update_kernel,
        out_shape=jax.ShapeDtypeStruct(params.shape, jnp.float32),
        scratch_shapes=[pltpu.VMEM((members + own, members), jnp.float32)],
        name="update",
    )(gram.reshape(members, members), cross, all_params.reshape(members, -1), params)


def shards(n_e, n_s, u, k, position, count, values, std, noise, params):
    up = [(i, i + 1) for i in range(n_s - 1)]
    down = [(i + 1, i) for i in range(n_s - 1)]
    ulo = lax.ppermute(u[:, -1], "space", up)
    klo = lax.ppermute(k[:, -1], "space", up)
    uhi = lax.ppermute(u[:, 0], "space", down)
    khi = lax.ppermute(k[:, 0], "space", down)
    pred = stencil(u, k)
    pred, picked = border(pred, u, k, ulo, klo, uhi, khi, position)
    gram, cross, all_params = products(n_e, n_s, count, picked, noise, values, std, params)
    return update(gram, cross, all_params, params), pred


def solution(mesh):
    in_specs = (
        P("ens", "space", None, None),
        P("ens", "space", None, None),
        P("space"),
        P("space"),
        P("space"),
        P("space"),
        P("ens", "space"),
        P("ens", "space"),
    )
    out_specs = (P("ens", "space"), P("ens", "space", None, None))
    body = functools.partial(shards, mesh.shape["ens"], mesh.shape["space"])
    return jax.shard_map(body, mesh=mesh, in_specs=in_specs, out_specs=out_specs, check_vma=False)
```

```python
import functools
import math

import jax
import jax.numpy as jnp
from jax import lax
from jax.experimental import pallas as pl
from jax.experimental.pallas import tpu as pltpu
from jax.sharding import PartitionSpec as P

half_step = 0.04
HI = lax.Precision.HIGHEST
MESH = pl.DeviceIdType.MESH


def stencil_kernel(u_ref, k_ref, o_ref, t_ref):
    members, cz, nx, ny = u_ref.shape
    row = lax.broadcasted_iota(jnp.int32, (nx, ny), 0)
    lane = lax.broadcasted_iota(jnp.int32, (nx, ny), 1)
    first_x, last_x = row == 0, row == nx - 1
    first_y, last_y = lane == 0, lane == ny - 1

    def member(m, carry):
        below = None
        u = u_ref[m, 0].astype(jnp.float32)
        k = k_ref[m, 0].astype(jnp.float32)
        for z in range(cz):
            ku = k * u
            fx = (k + pltpu.roll(k, nx - 1, 0)) * (pltpu.roll(u, nx - 1, 0) - u)
            total = jnp.where(last_x, -ku, fx) - jnp.where(first_x, ku, pltpu.roll(fx, 1, 0))
            fy = (k + pltpu.roll(k, ny - 1, 1)) * (pltpu.roll(u, ny - 1, 1) - u)
            total += jnp.where(last_y, -ku, fy) - jnp.where(first_y, ku, pltpu.roll(fy, 1, 1))
            if below is not None:
                total -= below
            if z < cz - 1:
                u_next = u_ref[m, z + 1].astype(jnp.float32)
                k_next = k_ref[m, z + 1].astype(jnp.float32)
                below = (k + k_next) * (u_next - u)
                total += below
            o_ref[m, z] = u + half_step * total
            if z < cz - 1:
                u, k = u_next, k_next
        return carry

    lax.fori_loop(0, members, member, 0)

    def turn(z, carry):
        for x in range(0, nx, 8):
            tile = o_ref[:, z, x : x + 8, :]
            t_ref[pl.ds(pl.multiple_of(z * nx, nx) + x, 8)] = jnp.swapaxes(tile, 0, 1)
        return carry

    lax.fori_loop(0, cz, turn, 0)


def stencil(u, k):
    m, cz, nx, ny = u.shape
    block = 8
    spec = pl.BlockSpec((block, cz, nx, ny), lambda g: (g, 0, 0, 0))
    return pl.pallas_call(
        stencil_kernel,
        grid=(m // block,),
        in_specs=[spec, spec],
        out_specs=[spec, pl.BlockSpec((cz * nx, block, ny), lambda g: (0, g, 0))],
        out_shape=[
            jax.ShapeDtypeStruct(u.shape, jnp.float32),
            jax.ShapeDtypeStruct((cz * nx, m, ny), jnp.float32),
        ],
        cost_estimate=pl.CostEstimate(
            flops=40 * u.size, bytes_accessed=8 * u.size, transcendentals=0
        ),
        name="stencil",
    )(u, k)


def border_kernel(
    row_ref, col_ref, p_ref, u_ref, k_ref, ulo_ref, klo_ref, uhi_ref, khi_ref, turned_ref,
    o_ref, picked_ref, scr, sem,
):
    g, e = pl.program_id(0), pl.program_id(1)
    block, _, nx, ny = p_ref.shape
    cells, members, _ = scr.shape
    inner = pl.ds(nx, cells - 2 * nx)
    load = pltpu.make_async_copy(turned_ref.at[inner], scr.at[inner], sem)
    u = u_ref[:, 0].astype(jnp.float32)
    k = k_ref[:, 0].astype(jnp.float32)
    own = pl.ds(pl.multiple_of(g * block, block), block)

    def fix(row, un_ref, kn_ref):
        un = un_ref[...].astype(jnp.float32)
        kn = kn_ref[...].astype(jnp.float32)
        new = p_ref[:, 0] + half_step * (k + kn) * (un - u)
        o_ref[:, 0] = new
        for x in range(0, nx, 8):
            scr[row + x : row + x + 8, own, :] = jnp.swapaxes(new[:, x : x + 8, :], 0, 1)

    @pl.when(jnp.logical_and(g == 0, e == 0))
    def _():
        load.start()

    @pl.when(e == 0)
    def _():
        fix(0, ulo_ref, klo_ref)

    @pl.when(e == 1)
    def _():
        fix(cells - nx, uhi_ref, khi_ref)

    @pl.when(jnp.logical_and(g == pl.num_programs(0) - 1, e == 1))
    def _():
        load.wait()
        lane = lax.broadcasted_iota(jnp.int32, (members, ny), 1)
        unroll = 8

        def chunk(c, carry):
            def step(s, acc):
                for i in range(unroll):
                    jj = s * unroll + i
                    j = c * ny + jj
                    v = pltpu.roll(scr[row_ref[j]], col_ref[j], 1)
                    acc = jnp.where(lane == jj, v, acc)
                return acc

            zero = jnp.zeros((members, ny), jnp.float32)
            acc = lax.fori_loop(0, ny // unroll, step, zero)
            picked_ref[:, pl.ds(pl.multiple_of(c * ny, ny), ny)] = acc
            return carry

        lax.fori_loop(0, picked_ref.shape[1] // ny, chunk, 0)


def border(pred, turned, u, k, ulo, klo, uhi, khi, position):
    m, cz, nx, ny = u.shape
    slots = position.shape[0]
    block = 8
    row = position // ny
    slot = jnp.arange(slots, dtype=jnp.int32)
    shift = (slot - position % ny) % ny
    edge = pl.BlockSpec((block, 1, nx, ny), lambda g, e, *_: (g, e * (cz - 1), 0, 0))
    halo = pl.BlockSpec((block, nx, ny), lambda g, e, *_: (g, 0, 0))
    return pl.pallas_call(
        border_kernel,
        grid_spec=pltpu.PrefetchScalarGridSpec(
            num_scalar_prefetch=2,
            grid=(m // block, 2),
            in_specs=[edge, edge, edge, halo, halo, halo, halo]
            + [pl.BlockSpec(memory_space=pl.ANY)],
            out_specs=[edge, pl.BlockSpec((m, slots), lambda g, e, *_: (0, 0))],
            scratch_shapes=[pltpu.VMEM(turned.shape, jnp.float32), pltpu.SemaphoreType.DMA],
        ),
        out_shape=[
            jax.ShapeDtypeStruct(u.shape, jnp.float32),
            jax.ShapeDtypeStruct((m, slots), jnp.float32),
        ],
        input_output_aliases={2: 0},
        name="border",
    )(row, shift, pred, u, k, ulo, klo, uhi, khi, turned)


def products_kernel(
    n_e, n_s, count_ref, picked_ref, noise_ref, values_ref, std_ref, params_ref,
    gram_ref, cross_ref, all_params_ref,
    all_picked, part, parts, total,
    send_a, recv_a, send_p, recv_p, send_s, recv_s, send_g, recv_g,
):
    own, slots = picked_ref.shape
    members = own * n_e
    me_e, me_s = lax.axis_index("ens"), lax.axis_index("space")
    scale = math.sqrt(members - 1.0)

    def ens_peer(d):
        return (lax.rem(me_e + d, n_e), me_s)

    def space_peer(d):
        return (me_e, lax.rem(me_s + d, n_s))

    barrier = pltpu.get_barrier_semaphore()
    for d in range(1, n_e):
        pl.semaphore_signal(barrier, inc=1, device_id=ens_peer(d), device_id_type=MESH)
    for d in range(1, n_s):
        pl.semaphore_signal(barrier, inc=1, device_id=space_peer(d), device_id_type=MESH)
    pl.semaphore_wait(barrier, n_e + n_s - 2)

    def send(src, dst, ssem, rsem, peer):
        copy = pltpu.make_async_remote_copy(
            src_ref=src, dst_ref=dst, send_sem=ssem, recv_sem=rsem,
            device_id=peer, device_id_type=MESH,
        )
        copy.start()
        return copy

    picked_copies = [
        send(picked_ref, all_picked.at[me_e], send_a.at[d], recv_a.at[d], ens_peer(d))
        for d in range(1, n_e)
    ]
    params_copies = [
        send(params_ref, all_params_ref.at[me_e], send_p.at[d], recv_p.at[d], ens_peer(d))
        for d in range(1, n_e)
    ]
    all_params_ref[me_e] = params_ref[...]
    mine = picked_ref[...]
    all_picked[me_e] = mine
    live = lax.broadcasted_iota(jnp.int32, (1, slots), 1) < count_ref[0]
    std = std_ref[...]
    inverse = jnp.where(live, 1.0 / (std * scale), 0.0)
    misfit = jnp.where(live, (values_ref[...] - mine) / std + noise_ref[...], 0.0)
    for copy in picked_copies:
        copy.wait()
    everyone = all_picked[...].reshape(members, slots)
    centre = jnp.sum(everyone, axis=0, keepdims=True) / members
    spread = (everyone - centre) * inverse
    left = jnp.concatenate([(mine - centre) * inverse, misfit], axis=0)
    part[...] = lax.dot_general(
        left, spread, (((1,), (1,)), ((), ())),
        precision=HI, preferred_element_type=jnp.float32,
    )
    space_copies = [
        send(part, parts.at[d], send_s.at[d], recv_s.at[d], space_peer(d)) for d in range(1, n_s)
    ]
    acc = part[...]
    for d in range(1, n_s):
        space_copies[d - 1].wait()
        acc += parts[d]
    total[...] = acc[:own]
    gram_copies = [
        send(total, gram_ref.at[me_e], send_g.at[d], recv_g.at[d], ens_peer(d))
        for d in range(1, n_e)
    ]
    gram_ref[me_e] = acc[:own]
    cross_ref[...] = acc[own:]
    for copy in gram_copies:
        copy.wait()
    for copy in params_copies:
        copy.wait()


def products(n_e, n_s, count, picked, noise, values, std, params):
    own, slots = picked.shape
    vmem = pl.BlockSpec(memory_space=pltpu.VMEM)
    dma = pltpu.SemaphoreType.DMA
    return pl.pallas_call(
        functools.partial(products_kernel, n_e, n_s),
        in_specs=[pl.BlockSpec(memory_space=pltpu.SMEM)] + [vmem] * 5,
        out_specs=[vmem] * 3,
        out_shape=[
            jax.ShapeDtypeStruct((n_e, own, n_e * own), jnp.float32),
            jax.ShapeDtypeStruct((own, n_e * own), jnp.float32),
            jax.ShapeDtypeStruct((n_e,) + params.shape, jnp.float32),
        ],
        scratch_shapes=[
            pltpu.VMEM((n_e, own, slots), jnp.float32),
            pltpu.VMEM((2 * own, n_e * own), jnp.float32),
            pltpu.VMEM((n_s, 2 * own, n_e * own), jnp.float32),
            pltpu.VMEM((own, n_e * own), jnp.float32),
        ]
        + [dma((n_e,))] * 4 + [dma((n_s,))] * 2 + [dma((n_e,))] * 2,
        compiler_params=pltpu.CompilerParams(collective_id=0, has_side_effects=True),
        name="products",
    )(count, picked, noise, values.reshape(1, -1), std.reshape(1, -1), params)


def update_kernel(gram_ref, cross_ref, all_params_ref, params_ref, o_ref, work):
    members = gram_ref.shape[1]
    own = cross_ref.shape[0]
    rows = lax.broadcasted_iota(jnp.int32, (members, members), 0)
    cols = lax.broadcasted_iota(jnp.int32, (members, members), 1)
    lane = lax.broadcasted_iota(jnp.int32, (1, members), 1)
    work[:members] = gram_ref[...] + jnp.where(rows == cols, 1.0, 0.0)
    work[members:] = cross_ref[...]

    pivots = 4

    def step(s, diagonal):
        first = s * pivots
        t = work[...]
        here = [lane == first + i for i in range(pivots)]
        columns = [
            jnp.sum(jnp.where(here[i], t, 0.0), axis=1, keepdims=True) for i in range(pivots)
        ]
        rows = [work[pl.ds(first + i, 1), :] for i in range(pivots)]
        corner = [
            [jnp.sum(jnp.where(here[j], rows[i], 0.0), axis=1, keepdims=True) for j in range(pivots)]
            for i in range(pivots)
        ]
        for i in range(pivots):
            pivot = corner[i][i]
            diagonal = jnp.where(here[i], pivot, diagonal)
            inverse = 1.0 / pivot
            factor = jnp.where(here[i], 0.0, rows[i] * inverse)
            t = t - columns[i] * factor
            for j in range(i + 1, pivots):
                ratio = corner[i][j] * inverse
                columns[j] = columns[j] - columns[i] * ratio
                rows[j] = rows[j] - corner[j][i] * factor
                for l in range(i + 1, pivots):
                    corner[l][j] = corner[l][j] - corner[l][i] * ratio
        work[...] = t
        return diagonal

    ones = jnp.ones((1, members), jnp.float32)
    diagonal = lax.fori_loop(0, members // pivots, step, ones)
    weights = work[members:] / diagonal
    all_params = all_params_ref[...]
    centre = jnp.sum(all_params, axis=0, keepdims=True) / members
    anomaly = (all_params - centre) / math.sqrt(members - 1.0)
    o_ref[...] = params_ref[...] + jnp.dot(
        weights, anomaly, precision=HI, preferred_element_type=jnp.float32
    )


def update(gram, cross, all_params, params):
    members, own = gram.shape[2], cross.shape[0]
    return pl.pallas_call(
        update_kernel,
        out_shape=jax.ShapeDtypeStruct(params.shape, jnp.float32),
        scratch_shapes=[pltpu.VMEM((members + own, members), jnp.float32)],
        name="update",
    )(gram.reshape(members, members), cross, all_params.reshape(members, -1), params)


def shards(n_e, n_s, u, k, position, count, values, std, noise, params):
    up = [(i, i + 1) for i in range(n_s - 1)]
    down = [(i + 1, i) for i in range(n_s - 1)]
    ulo = lax.ppermute(u[:, -1], "space", up)
    klo = lax.ppermute(k[:, -1], "space", up)
    uhi = lax.ppermute(u[:, 0], "space", down)
    khi = lax.ppermute(k[:, 0], "space", down)
    pred, turned = stencil(u, k)
    pred, picked = border(pred, turned, u, k, ulo, klo, uhi, khi, position)
    gram, cross, all_params = products(n_e, n_s, count, picked, noise, values, std, params)
    return update(gram, cross, all_params, params), pred


def solution(mesh):
    in_specs = (
        P("ens", "space", None, None),
        P("ens", "space", None, None),
        P("space"),
        P("space"),
        P("space"),
        P("space"),
        P("ens", "space"),
        P("ens", "space"),
    )
    out_specs = (P("ens", "space"), P("ens", "space", None, None))
    body = functools.partial(shards, mesh.shape["ens"], mesh.shape["space"])
    return jax.shard_map(body, mesh=mesh, in_specs=in_specs, out_specs=out_specs, check_vma=False)
```

```python
import functools
import math

import jax
import jax.numpy as jnp
from jax import lax
from jax.experimental import pallas as pl
from jax.experimental.pallas import tpu as pltpu
from jax.sharding import PartitionSpec as P

half_step = 0.04
HI = lax.Precision.HIGHEST
MESH = pl.DeviceIdType.MESH


def stencil_kernel(u_ref, k_ref, o_ref, t_ref):
    members, cz, nx, ny = u_ref.shape
    row = lax.broadcasted_iota(jnp.int32, (nx, ny), 0)
    lane = lax.broadcasted_iota(jnp.int32, (nx, ny), 1)
    first_x, last_x = row == 0, row == nx - 1
    first_y, last_y = lane == 0, lane == ny - 1

    def member(m, carry):
        below = None
        u = u_ref[m, 0].astype(jnp.float32)
        k = k_ref[m, 0].astype(jnp.float32)
        for z in range(cz):
            ku = k * u
            fx = (k + pltpu.roll(k, nx - 1, 0)) * (pltpu.roll(u, nx - 1, 0) - u)
            total = jnp.where(last_x, -ku, fx) - jnp.where(first_x, ku, pltpu.roll(fx, 1, 0))
            fy = (k + pltpu.roll(k, ny - 1, 1)) * (pltpu.roll(u, ny - 1, 1) - u)
            total += jnp.where(last_y, -ku, fy) - jnp.where(first_y, ku, pltpu.roll(fy, 1, 1))
            if below is not None:
                total -= below
            if z < cz - 1:
                u_next = u_ref[m, z + 1].astype(jnp.float32)
                k_next = k_ref[m, z + 1].astype(jnp.float32)
                below = (k + k_next) * (u_next - u)
                total += below
            o_ref[m, z] = u + half_step * total
            if z < cz - 1:
                u, k = u_next, k_next
        return carry

    lax.fori_loop(0, members, member, 0)

    def turn(z, carry):
        for x in range(0, nx, 8):
            tile = o_ref[:, z, x : x + 8, :]
            t_ref[pl.ds(pl.multiple_of(z * nx, nx) + x, 8)] = jnp.swapaxes(tile, 0, 1)
        return carry

    lax.fori_loop(0, cz, turn, 0)


def stencil(u, k):
    m, cz, nx, ny = u.shape
    block = 8
    spec = pl.BlockSpec((block, cz, nx, ny), lambda g: (g, 0, 0, 0))
    return pl.pallas_call(
        stencil_kernel,
        grid=(m // block,),
        in_specs=[spec, spec],
        out_specs=[spec, pl.BlockSpec((cz * nx, block, ny), lambda g: (0, g, 0))],
        out_shape=[
            jax.ShapeDtypeStruct(u.shape, jnp.float32),
            jax.ShapeDtypeStruct((cz * nx, m, ny), jnp.float32),
        ],
        cost_estimate=pl.CostEstimate(
            flops=40 * u.size, bytes_accessed=8 * u.size, transcendentals=0
        ),
        name="stencil",
    )(u, k)


def border_kernel(
    row_ref, col_ref, p_ref, u_ref, k_ref, turned_ref, ulo_ref, klo_ref, uhi_ref, khi_ref,
    o_ref, picked_ref, scr, edge, u_own, k_own, sem,
):
    cells, members, ny = scr.shape
    nx = edge.shape[2]
    cz = cells // nx
    last = cz - 1
    tile = 16

    def start(src, dst, i):
        copy = pltpu.make_async_copy(src, dst, sem.at[i])
        copy.start()
        return copy

    edges = [
        [
            start(p_ref.at[:, z], edge.at[e], 3 * e),
            start(u_ref.at[:, z], u_own.at[e], 3 * e + 1),
            start(k_ref.at[:, z], k_own.at[e], 3 * e + 2),
        ]
        for e, z in enumerate((0, last))
    ]
    inner = pl.ds(nx, cells - 2 * nx)
    load = start(turned_ref.at[inner], scr.at[inner], 6)
    stores = []
    for e, (z, un_ref, kn_ref) in enumerate(((0, ulo_ref, klo_ref), (last, uhi_ref, khi_ref))):
        for copy in edges[e]:
            copy.wait()

        def fix(t, carry):
            x = pl.multiple_of(t * tile, tile)
            for m in range(0, members, 8):
                at = (pl.ds(m, 8), pl.ds(x, tile), slice(None))
                u = u_own[(e,) + at].astype(jnp.float32)
                k = k_own[(e,) + at].astype(jnp.float32)
                un = un_ref[at].astype(jnp.float32)
                kn = kn_ref[at].astype(jnp.float32)
                new = edge[(e,) + at] + half_step * (k + kn) * (un - u)
                edge[(e,) + at] = new
                for i in range(0, tile, 8):
                    turned = jnp.swapaxes(new[:, i : i + 8, :], 0, 1)
                    scr[pl.ds(z * nx + x + i, 8), m : m + 8, :] = turned
            return carry

        lax.fori_loop(0, nx // tile, fix, 0)
        stores.append(start(edge.at[e], o_ref.at[:, z], 7 + e))
    load.wait()
    lane = lax.broadcasted_iota(jnp.int32, (members, ny), 1)
    unroll = 32

    def chunk(c, carry):
        def step(s, acc):
            for i in range(unroll):
                jj = s * unroll + i
                j = c * ny + jj
                v = pltpu.roll(scr[row_ref[j]], col_ref[j], 1)
                acc = jnp.where(lane == jj, v, acc)
            return acc

        acc = lax.fori_loop(0, ny // unroll, step, jnp.zeros((members, ny), jnp.float32))
        picked_ref[:, pl.ds(pl.multiple_of(c * ny, ny), ny)] = acc
        return carry

    lax.fori_loop(0, picked_ref.shape[1] // ny, chunk, 0)
    for copy in stores:
        copy.wait()


def border(pred, turned, u, k, ulo, klo, uhi, khi, position):
    m, cz, nx, ny = u.shape
    slots = position.shape[0]
    row = position // ny
    slot = jnp.arange(slots, dtype=jnp.int32)
    shift = (slot - position % ny) % ny
    smem = pl.BlockSpec(memory_space=pltpu.SMEM)
    vmem = pl.BlockSpec(memory_space=pltpu.VMEM)
    whole = pl.BlockSpec(memory_space=pl.ANY)
    return pl.pallas_call(
        border_kernel,
        in_specs=[smem, smem] + [whole] * 4 + [vmem] * 4,
        out_specs=[whole, vmem],
        out_shape=[
            jax.ShapeDtypeStruct(u.shape, jnp.float32),
            jax.ShapeDtypeStruct((m, slots), jnp.float32),
        ],
        scratch_shapes=[
            pltpu.VMEM(turned.shape, jnp.float32),
            pltpu.VMEM((2, m, nx, ny), jnp.float32),
            pltpu.VMEM((2, m, nx, ny), u.dtype),
            pltpu.VMEM((2, m, nx, ny), u.dtype),
            pltpu.SemaphoreType.DMA((9,)),
        ],
        input_output_aliases={2: 0},
        name="border",
    )(row, shift, pred, u, k, turned, ulo, klo, uhi, khi)


def products_kernel(
    n_e, n_s, count_ref, picked_ref, noise_ref, values_ref, std_ref, params_ref,
    gram_ref, cross_ref, all_params_ref,
    all_picked, part, parts, total,
    send_a, recv_a, send_p, recv_p, send_s, recv_s, send_g, recv_g,
):
    own, slots = picked_ref.shape
    members = own * n_e
    me_e, me_s = lax.axis_index("ens"), lax.axis_index("space")
    scale = math.sqrt(members - 1.0)

    def ens_peer(d):
        return (lax.rem(me_e + d, n_e), me_s)

    def space_peer(d):
        return (me_e, lax.rem(me_s + d, n_s))

    barrier = pltpu.get_barrier_semaphore()
    for d in range(1, n_e):
        pl.semaphore_signal(barrier, inc=1, device_id=ens_peer(d), device_id_type=MESH)
    for d in range(1, n_s):
        pl.semaphore_signal(barrier, inc=1, device_id=space_peer(d), device_id_type=MESH)
    pl.semaphore_wait(barrier, n_e + n_s - 2)

    def send(src, dst, ssem, rsem, peer):
        copy = pltpu.make_async_remote_copy(
            src_ref=src, dst_ref=dst, send_sem=ssem, recv_sem=rsem,
            device_id=peer, device_id_type=MESH,
        )
        copy.start()
        return copy

    picked_copies = [
        send(picked_ref, all_picked.at[me_e], send_a.at[d], recv_a.at[d], ens_peer(d))
        for d in range(1, n_e)
    ]
    params_copies = [
        send(params_ref, all_params_ref.at[me_e], send_p.at[d], recv_p.at[d], ens_peer(d))
        for d in range(1, n_e)
    ]
    all_params_ref[me_e] = params_ref[...]
    mine = picked_ref[...]
    all_picked[me_e] = mine
    live = lax.broadcasted_iota(jnp.int32, (1, slots), 1) < count_ref[0]
    std = std_ref[...]
    inverse = jnp.where(live, 1.0 / (std * scale), 0.0)
    misfit = jnp.where(live, (values_ref[...] - mine) / std + noise_ref[...], 0.0)
    for copy in picked_copies:
        copy.wait()
    everyone = all_picked[...].reshape(members, slots)
    centre = jnp.sum(everyone, axis=0, keepdims=True) / members
    spread = (everyone - centre) * inverse
    left = jnp.concatenate([(mine - centre) * inverse, misfit], axis=0)
    part[...] = lax.dot_general(
        left, spread, (((1,), (1,)), ((), ())),
        precision=HI, preferred_element_type=jnp.float32,
    )
    space_copies = [
        send(part, parts.at[d], send_s.at[d], recv_s.at[d], space_peer(d)) for d in range(1, n_s)
    ]
    acc = part[...]
    for d in range(1, n_s):
        space_copies[d - 1].wait()
        acc += parts[d]
    total[...] = acc[:own]
    gram_copies = [
        send(total, gram_ref.at[me_e], send_g.at[d], recv_g.at[d], ens_peer(d))
        for d in range(1, n_e)
    ]
    gram_ref[me_e] = acc[:own]
    cross_ref[...] = acc[own:]
    for copy in gram_copies:
        copy.wait()
    for copy in params_copies:
        copy.wait()


def products(n_e, n_s, count, picked, noise, values, std, params):
    own, slots = picked.shape
    vmem = pl.BlockSpec(memory_space=pltpu.VMEM)
    dma = pltpu.SemaphoreType.DMA
    return pl.pallas_call(
        functools.partial(products_kernel, n_e, n_s),
        in_specs=[pl.BlockSpec(memory_space=pltpu.SMEM)] + [vmem] * 5,
        out_specs=[vmem] * 3,
        out_shape=[
            jax.ShapeDtypeStruct((n_e, own, n_e * own), jnp.float32),
            jax.ShapeDtypeStruct((own, n_e * own), jnp.float32),
            jax.ShapeDtypeStruct((n_e,) + params.shape, jnp.float32),
        ],
        scratch_shapes=[
            pltpu.VMEM((n_e, own, slots), jnp.float32),
            pltpu.VMEM((2 * own, n_e * own), jnp.float32),
            pltpu.VMEM((n_s, 2 * own, n_e * own), jnp.float32),
            pltpu.VMEM((own, n_e * own), jnp.float32),
        ]
        + [dma((n_e,))] * 4 + [dma((n_s,))] * 2 + [dma((n_e,))] * 2,
        compiler_params=pltpu.CompilerParams(collective_id=0, has_side_effects=True),
        name="products",
    )(count, picked, noise, values.reshape(1, -1), std.reshape(1, -1), params)


def update_kernel(gram_ref, cross_ref, all_params_ref, params_ref, o_ref, work):
    members = gram_ref.shape[1]
    own = cross_ref.shape[0]
    rows = lax.broadcasted_iota(jnp.int32, (members, members), 0)
    cols = lax.broadcasted_iota(jnp.int32, (members, members), 1)
    lane = lax.broadcasted_iota(jnp.int32, (1, members), 1)
    work[:members] = gram_ref[...] + jnp.where(rows == cols, 1.0, 0.0)
    work[members:] = cross_ref[...]

    pivots = 4

    def step(s, diagonal):
        first = s * pivots
        t = work[...]
        here = [lane == first + i for i in range(pivots)]
        columns = [
            jnp.sum(jnp.where(here[i], t, 0.0), axis=1, keepdims=True) for i in range(pivots)
        ]
        rows = [work[pl.ds(first + i, 1), :] for i in range(pivots)]
        corner = [
            [jnp.sum(jnp.where(here[j], rows[i], 0.0), axis=1, keepdims=True) for j in range(pivots)]
            for i in range(pivots)
        ]
        for i in range(pivots):
            pivot = corner[i][i]
            diagonal = jnp.where(here[i], pivot, diagonal)
            inverse = 1.0 / pivot
            factor = jnp.where(here[i], 0.0, rows[i] * inverse)
            t = t - columns[i] * factor
            for j in range(i + 1, pivots):
                ratio = corner[i][j] * inverse
                columns[j] = columns[j] - columns[i] * ratio
                rows[j] = rows[j] - corner[j][i] * factor
                for l in range(i + 1, pivots):
                    corner[l][j] = corner[l][j] - corner[l][i] * ratio
        work[...] = t
        return diagonal

    ones = jnp.ones((1, members), jnp.float32)
    diagonal = lax.fori_loop(0, members // pivots, step, ones)
    weights = work[members:] / diagonal
    all_params = all_params_ref[...]
    centre = jnp.sum(all_params, axis=0, keepdims=True) / members
    anomaly = (all_params - centre) / math.sqrt(members - 1.0)
    o_ref[...] = params_ref[...] + jnp.dot(
        weights, anomaly, precision=HI, preferred_element_type=jnp.float32
    )


def update(gram, cross, all_params, params):
    members, own = gram.shape[2], cross.shape[0]
    return pl.pallas_call(
        update_kernel,
        out_shape=jax.ShapeDtypeStruct(params.shape, jnp.float32),
        scratch_shapes=[pltpu.VMEM((members + own, members), jnp.float32)],
        name="update",
    )(gram.reshape(members, members), cross, all_params.reshape(members, -1), params)


def shards(n_e, n_s, u, k, position, count, values, std, noise, params):
    up = [(i, i + 1) for i in range(n_s - 1)]
    down = [(i + 1, i) for i in range(n_s - 1)]
    ulo = lax.ppermute(u[:, -1], "space", up)
    klo = lax.ppermute(k[:, -1], "space", up)
    uhi = lax.ppermute(u[:, 0], "space", down)
    khi = lax.ppermute(k[:, 0], "space", down)
    pred, turned = stencil(u, k)
    pred, picked = border(pred, turned, u, k, ulo, klo, uhi, khi, position)
    gram, cross, all_params = products(n_e, n_s, count, picked, noise, values, std, params)
    return update(gram, cross, all_params, params), pred


def solution(mesh):
    in_specs = (
        P("ens", "space", None, None),
        P("ens", "space", None, None),
        P("space"),
        P("space"),
        P("space"),
        P("space"),
        P("ens", "space"),
        P("ens", "space"),
    )
    out_specs = (P("ens", "space"), P("ens", "space", None, None))
    body = functools.partial(shards, mesh.shape["ens"], mesh.shape["space"])
    return jax.shard_map(body, mesh=mesh, in_specs=in_specs, out_specs=out_specs, check_vma=False)
```

```python
import functools
import math

import jax
import jax.numpy as jnp
from jax import lax
from jax.experimental import pallas as pl
from jax.experimental.pallas import tpu as pltpu
from jax.sharding import PartitionSpec as P

half_step = 0.04
HI = lax.Precision.HIGHEST
MESH = pl.DeviceIdType.MESH


def stencil_kernel(u_ref, k_ref, o_ref, t_ref):
    members, cz, nx, ny = u_ref.shape
    row = lax.broadcasted_iota(jnp.int32, (nx, ny), 0)
    lane = lax.broadcasted_iota(jnp.int32, (nx, ny), 1)
    first_x, last_x = row == 0, row == nx - 1
    first_y, last_y = lane == 0, lane == ny - 1

    def member(m, carry):
        below = None
        u = u_ref[m, 0].astype(jnp.float32)
        k = k_ref[m, 0].astype(jnp.float32)
        for z in range(cz):
            ku = k * u
            fx = (k + pltpu.roll(k, nx - 1, 0)) * (pltpu.roll(u, nx - 1, 0) - u)
            total = jnp.where(last_x, -ku, fx) - jnp.where(first_x, ku, pltpu.roll(fx, 1, 0))
            fy = (k + pltpu.roll(k, ny - 1, 1)) * (pltpu.roll(u, ny - 1, 1) - u)
            total += jnp.where(last_y, -ku, fy) - jnp.where(first_y, ku, pltpu.roll(fy, 1, 1))
            if below is not None:
                total -= below
            if z < cz - 1:
                u_next = u_ref[m, z + 1].astype(jnp.float32)
                k_next = k_ref[m, z + 1].astype(jnp.float32)
                below = (k + k_next) * (u_next - u)
                total += below
            o_ref[m, z] = u + half_step * total
            if z < cz - 1:
                u, k = u_next, k_next
        return carry

    lax.fori_loop(0, members, member, 0)

    def turn(z, carry):
        for x in range(0, nx, 8):
            tile = o_ref[:, z, x : x + 8, :]
            t_ref[pl.ds(pl.multiple_of(z * nx, nx) + x, 8)] = jnp.swapaxes(tile, 0, 1)
        return carry

    lax.fori_loop(0, cz, turn, 0)


def stencil(u, k):
    m, cz, nx, ny = u.shape
    block = 8
    spec = pl.BlockSpec((block, cz, nx, ny), lambda g: (g, 0, 0, 0))
    return pl.pallas_call(
        stencil_kernel,
        grid=(m // block,),
        in_specs=[spec, spec],
        out_specs=[spec, pl.BlockSpec((cz * nx, block, ny), lambda g: (0, g, 0))],
        out_shape=[
            jax.ShapeDtypeStruct(u.shape, jnp.float32),
            jax.ShapeDtypeStruct((cz * nx, m, ny), jnp.float32),
        ],
        cost_estimate=pl.CostEstimate(
            flops=40 * u.size, bytes_accessed=8 * u.size, transcendentals=0
        ),
        name="stencil",
    )(u, k)


def border_kernel(
    row_ref, col_ref, p_ref, u_ref, k_ref, turned_ref, ulo_ref, klo_ref, uhi_ref, khi_ref,
    o_ref, picked_ref, scr, edge, u_own, k_own, sem,
):
    cells, members, ny = scr.shape
    nx = edge.shape[2]
    cz = cells // nx
    last = cz - 1
    tile = 16

    def start(src, dst, i):
        copy = pltpu.make_async_copy(src, dst, sem.at[i])
        copy.start()
        return copy

    edges = [
        [
            start(p_ref.at[:, z], edge.at[e], 3 * e),
            start(u_ref.at[:, z], u_own.at[e], 3 * e + 1),
            start(k_ref.at[:, z], k_own.at[e], 3 * e + 2),
        ]
        for e, z in enumerate((0, last))
    ]
    inner = pl.ds(nx, cells - 2 * nx)
    load = start(turned_ref.at[inner], scr.at[inner], 6)
    stores = []
    for e, (z, un_ref, kn_ref) in enumerate(((0, ulo_ref, klo_ref), (last, uhi_ref, khi_ref))):
        for copy in edges[e]:
            copy.wait()

        def fix(t, carry):
            x = pl.multiple_of(t * tile, tile)
            for m in range(0, members, 8):
                at = (pl.ds(m, 8), pl.ds(x, tile), slice(None))
                u = u_own[(e,) + at].astype(jnp.float32)
                k = k_own[(e,) + at].astype(jnp.float32)
                un = un_ref[at].astype(jnp.float32)
                kn = kn_ref[at].astype(jnp.float32)
                new = edge[(e,) + at] + half_step * (k + kn) * (un - u)
                edge[(e,) + at] = new
                for i in range(0, tile, 8):
                    turned = jnp.swapaxes(new[:, i : i + 8, :], 0, 1)
                    scr[pl.ds(z * nx + x + i, 8), m : m + 8, :] = turned
            return carry

        lax.fori_loop(0, nx // tile, fix, 0)
        stores.append(start(edge.at[e], o_ref.at[:, z], 7 + e))
    load.wait()
    lane = lax.broadcasted_iota(jnp.int32, (members, ny), 1)
    unroll = 32

    def chunk(c, carry):
        def step(s, acc):
            for i in range(unroll):
                jj = s * unroll + i
                j = c * ny + jj
                v = pltpu.roll(scr[row_ref[j]], col_ref[j], 1)
                acc = jnp.where(lane == jj, v, acc)
            return acc

        acc = lax.fori_loop(0, ny // unroll, step, jnp.zeros((members, ny), jnp.float32))
        picked_ref[:, pl.ds(pl.multiple_of(c * ny, ny), ny)] = acc
        return carry

    lax.fori_loop(0, picked_ref.shape[1] // ny, chunk, 0)
    for copy in stores:
        copy.wait()


def border(pred, turned, u, k, ulo, klo, uhi, khi, position):
    m, cz, nx, ny = u.shape
    slots = position.shape[0]
    row = position // ny
    slot = jnp.arange(slots, dtype=jnp.int32)
    shift = (slot - position % ny) % ny
    smem = pl.BlockSpec(memory_space=pltpu.SMEM)
    vmem = pl.BlockSpec(memory_space=pltpu.VMEM)
    whole = pl.BlockSpec(memory_space=pl.ANY)
    return pl.pallas_call(
        border_kernel,
        in_specs=[smem, smem] + [whole] * 4 + [vmem] * 4,
        out_specs=[whole, vmem],
        out_shape=[
            jax.ShapeDtypeStruct(u.shape, jnp.float32),
            jax.ShapeDtypeStruct((m, slots), jnp.float32),
        ],
        scratch_shapes=[
            pltpu.VMEM(turned.shape, jnp.float32),
            pltpu.VMEM((2, m, nx, ny), jnp.float32),
            pltpu.VMEM((2, m, nx, ny), u.dtype),
            pltpu.VMEM((2, m, nx, ny), u.dtype),
            pltpu.SemaphoreType.DMA((9,)),
        ],
        input_output_aliases={2: 0},
        name="border",
    )(row, shift, pred, u, k, turned, ulo, klo, uhi, khi)


def products_kernel(
    n_e, n_s, count_ref, picked_ref, noise_ref, values_ref, std_ref, params_ref,
    gram_ref, cross_ref, all_params_ref,
    all_picked, part, parts, total,
    send_a, recv_a, send_h, recv_h, send_p, recv_p, send_s, recv_s, send_g, recv_g,
):
    own, slots = picked_ref.shape
    members = own * n_e
    me_e, me_s = lax.axis_index("ens"), lax.axis_index("space")
    scale = math.sqrt(members - 1.0)

    def ens_peer(d):
        return (lax.rem(me_e + d, n_e), me_s)

    def space_peer(d):
        return (me_e, lax.rem(me_s + d, n_s))

    barrier = pltpu.get_barrier_semaphore()
    for d in range(1, n_e):
        pl.semaphore_signal(barrier, inc=1, device_id=ens_peer(d), device_id_type=MESH)
    for d in range(1, n_s):
        pl.semaphore_signal(barrier, inc=1, device_id=space_peer(d), device_id_type=MESH)
    pl.semaphore_wait(barrier, n_e + n_s - 2)

    def send(src, dst, ssem, rsem, peer):
        copy = pltpu.make_async_remote_copy(
            src_ref=src, dst_ref=dst, send_sem=ssem, recv_sem=rsem,
            device_id=peer, device_id_type=MESH,
        )
        copy.start()
        return copy

    pair = me_e + 1 - 2 * lax.rem(me_e, 2)
    partner = (pair, me_s)
    hops = n_e // 2
    handed = [send(picked_ref, all_picked.at[me_e], send_h.at[0], recv_h.at[0], partner)]
    picked_copies = [
        send(picked_ref, all_picked.at[me_e], send_a.at[d], recv_a.at[d], ens_peer(2 * d))
        for d in range(1, hops)
    ]
    params_copies = [
        send(params_ref, all_params_ref.at[me_e], send_p.at[d], recv_p.at[d], ens_peer(d))
        for d in range(1, n_e)
    ]
    all_params_ref[me_e] = params_ref[...]
    mine = picked_ref[...]
    all_picked[me_e] = mine
    live = lax.broadcasted_iota(jnp.int32, (1, slots), 1) < count_ref[0]
    std = std_ref[...]
    inverse = jnp.where(live, 1.0 / (std * scale), 0.0)
    misfit = jnp.where(live, (values_ref[...] - mine) / std + noise_ref[...], 0.0)
    for d in range(1, hops):
        picked_copies[d - 1].wait()
        block = all_picked.at[lax.rem(me_e + n_e - 2 * d, n_e)]
        handed.append(send(block, block, send_h.at[d], recv_h.at[d], partner))
    for copy in handed:
        copy.wait()
    everyone = all_picked[...].reshape(members, slots)
    centre = jnp.sum(everyone, axis=0, keepdims=True) / members
    spread = (everyone - centre) * inverse
    left = jnp.concatenate([(mine - centre) * inverse, misfit], axis=0)
    part[...] = lax.dot_general(
        left, spread, (((1,), (1,)), ((), ())),
        precision=HI, preferred_element_type=jnp.float32,
    )
    space_copies = [
        send(part, parts.at[d], send_s.at[d], recv_s.at[d], space_peer(d)) for d in range(1, n_s)
    ]
    acc = part[...]
    for d in range(1, n_s):
        space_copies[d - 1].wait()
        acc += parts[d]
    total[...] = acc[:own]
    gram_copies = [
        send(total, gram_ref.at[me_e], send_g.at[d], recv_g.at[d], ens_peer(d))
        for d in range(1, n_e)
    ]
    gram_ref[me_e] = acc[:own]
    cross_ref[...] = acc[own:]
    for copy in gram_copies:
        copy.wait()
    for copy in params_copies:
        copy.wait()


def products(n_e, n_s, count, picked, noise, values, std, params):
    own, slots = picked.shape
    vmem = pl.BlockSpec(memory_space=pltpu.VMEM)
    dma = pltpu.SemaphoreType.DMA
    return pl.pallas_call(
        functools.partial(products_kernel, n_e, n_s),
        in_specs=[pl.BlockSpec(memory_space=pltpu.SMEM)] + [vmem] * 5,
        out_specs=[vmem] * 3,
        out_shape=[
            jax.ShapeDtypeStruct((n_e, own, n_e * own), jnp.float32),
            jax.ShapeDtypeStruct((own, n_e * own), jnp.float32),
            jax.ShapeDtypeStruct((n_e,) + params.shape, jnp.float32),
        ],
        scratch_shapes=[
            pltpu.VMEM((n_e, own, slots), jnp.float32),
            pltpu.VMEM((2 * own, n_e * own), jnp.float32),
            pltpu.VMEM((n_s, 2 * own, n_e * own), jnp.float32),
            pltpu.VMEM((own, n_e * own), jnp.float32),
        ]
        + [dma((n_e,))] * 6 + [dma((n_s,))] * 2 + [dma((n_e,))] * 2,
        compiler_params=pltpu.CompilerParams(collective_id=0, has_side_effects=True),
        name="products",
    )(count, picked, noise, values.reshape(1, -1), std.reshape(1, -1), params)


def update_kernel(gram_ref, cross_ref, all_params_ref, params_ref, o_ref, work):
    members = gram_ref.shape[1]
    own = cross_ref.shape[0]
    rows = lax.broadcasted_iota(jnp.int32, (members, members), 0)
    cols = lax.broadcasted_iota(jnp.int32, (members, members), 1)
    lane = lax.broadcasted_iota(jnp.int32, (1, members), 1)
    work[:members] = gram_ref[...] + jnp.where(rows == cols, 1.0, 0.0)
    work[members:] = cross_ref[...]

    pivots = 8
    segments = 4
    span = members // segments

    def step(lo, s, diagonal):
        first = lo + s * pivots
        t = work[lo:]
        here = [lane == first + i for i in range(pivots)]
        columns = [
            jnp.sum(jnp.where(here[i], t, 0.0), axis=1, keepdims=True) for i in range(pivots)
        ]
        rows = [work[pl.ds(first + i, 1), :] for i in range(pivots)]
        corner = [
            [jnp.sum(jnp.where(here[j], rows[i], 0.0), axis=1, keepdims=True) for j in range(pivots)]
            for i in range(pivots)
        ]
        for i in range(pivots):
            pivot = corner[i][i]
            diagonal = jnp.where(here[i], pivot, diagonal)
            inverse = 1.0 / pivot
            factor = jnp.where(here[i], 0.0, rows[i] * inverse)
            t = t - columns[i] * factor
            for j in range(i + 1, pivots):
                ratio = corner[i][j] * inverse
                columns[j] = columns[j] - columns[i] * ratio
                rows[j] = rows[j] - corner[j][i] * factor
                for l in range(i + 1, pivots):
                    corner[l][j] = corner[l][j] - corner[l][i] * ratio
        work[lo:] = t
        return diagonal

    diagonal = jnp.ones((1, members), jnp.float32)
    for part in range(segments):
        diagonal = lax.fori_loop(
            0, span // pivots, functools.partial(step, part * span), diagonal
        )
    weights = work[members:] / diagonal
    all_params = all_params_ref[...]
    centre = jnp.sum(all_params, axis=0, keepdims=True) / members
    anomaly = (all_params - centre) / math.sqrt(members - 1.0)
    o_ref[...] = params_ref[...] + jnp.dot(
        weights, anomaly, precision=HI, preferred_element_type=jnp.float32
    )


def update(gram, cross, all_params, params):
    members, own = gram.shape[2], cross.shape[0]
    return pl.pallas_call(
        update_kernel,
        out_shape=jax.ShapeDtypeStruct(params.shape, jnp.float32),
        scratch_shapes=[pltpu.VMEM((members + own, members), jnp.float32)],
        name="update",
    )(gram.reshape(members, members), cross, all_params.reshape(members, -1), params)


def shards(n_e, n_s, u, k, position, count, values, std, noise, params):
    up = [(i, i + 1) for i in range(n_s - 1)]
    down = [(i + 1, i) for i in range(n_s - 1)]
    ulo = lax.ppermute(u[:, -1], "space", up)
    klo = lax.ppermute(k[:, -1], "space", up)
    uhi = lax.ppermute(u[:, 0], "space", down)
    khi = lax.ppermute(k[:, 0], "space", down)
    pred, turned = stencil(u, k)
    pred, picked = border(pred, turned, u, k, ulo, klo, uhi, khi, position)
    gram, cross, all_params = products(n_e, n_s, count, picked, noise, values, std, params)
    return update(gram, cross, all_params, params), pred


def solution(mesh):
    in_specs = (
        P("ens", "space", None, None),
        P("ens", "space", None, None),
        P("space"),
        P("space"),
        P("space"),
        P("space"),
        P("ens", "space"),
        P("ens", "space"),
    )
    out_specs = (P("ens", "space"), P("ens", "space", None, None))
    body = functools.partial(shards, mesh.shape["ens"], mesh.shape["space"])
    return jax.shard_map(body, mesh=mesh, in_specs=in_specs, out_specs=out_specs, check_vma=False)
```

```python
import functools
import math

import jax
import jax.numpy as jnp
from jax import lax
from jax.experimental import pallas as pl
from jax.experimental.pallas import tpu as pltpu
from jax.sharding import PartitionSpec as P

half_step = 0.04
HI = lax.Precision.HIGHEST
MESH = pl.DeviceIdType.MESH


def stencil_kernel(u_ref, k_ref, o_ref, t_ref):
    members, cz, nx, ny = u_ref.shape
    row = lax.broadcasted_iota(jnp.int32, (nx, ny), 0)
    lane = lax.broadcasted_iota(jnp.int32, (nx, ny), 1)
    first_x, last_x = row == 0, row == nx - 1
    first_y, last_y = lane == 0, lane == ny - 1

    def member(m, carry):
        below = None
        u = u_ref[m, 0].astype(jnp.float32)
        k = k_ref[m, 0].astype(jnp.float32)
        for z in range(cz):
            ku = k * u
            fx = (k + pltpu.roll(k, nx - 1, 0)) * (pltpu.roll(u, nx - 1, 0) - u)
            total = jnp.where(last_x, -ku, fx) - jnp.where(first_x, ku, pltpu.roll(fx, 1, 0))
            fy = (k + pltpu.roll(k, ny - 1, 1)) * (pltpu.roll(u, ny - 1, 1) - u)
            total += jnp.where(last_y, -ku, fy) - jnp.where(first_y, ku, pltpu.roll(fy, 1, 1))
            if below is not None:
                total -= below
            if z < cz - 1:
                u_next = u_ref[m, z + 1].astype(jnp.float32)
                k_next = k_ref[m, z + 1].astype(jnp.float32)
                below = (k + k_next) * (u_next - u)
                total += below
            o_ref[m, z] = u + half_step * total
            if z < cz - 1:
                u, k = u_next, k_next
        return carry

    lax.fori_loop(0, members, member, 0)

    def turn(z, carry):
        for x in range(0, nx, 8):
            tile = o_ref[:, z, x : x + 8, :]
            t_ref[pl.ds(pl.multiple_of(z * nx, nx) + x, 8)] = jnp.swapaxes(tile, 0, 1)
        return carry

    lax.fori_loop(0, cz, turn, 0)


def stencil(u, k):
    m, cz, nx, ny = u.shape
    block = 8
    spec = pl.BlockSpec((block, cz, nx, ny), lambda g: (g, 0, 0, 0))
    return pl.pallas_call(
        stencil_kernel,
        grid=(m // block,),
        in_specs=[spec, spec],
        out_specs=[spec, pl.BlockSpec((cz * nx, block, ny), lambda g: (0, g, 0))],
        out_shape=[
            jax.ShapeDtypeStruct(u.shape, jnp.float32),
            jax.ShapeDtypeStruct((cz * nx, m, ny), jnp.float32),
        ],
        cost_estimate=pl.CostEstimate(
            flops=40 * u.size, bytes_accessed=8 * u.size, transcendentals=0
        ),
        name="stencil",
    )(u, k)


def border_kernel(
    row_ref, col_ref, p_ref, u_ref, k_ref, turned_ref, ulo_ref, klo_ref, uhi_ref, khi_ref,
    o_ref, picked_ref, scr, edge, u_own, k_own, sem,
):
    cells, members, ny = scr.shape
    nx = edge.shape[2]
    cz = cells // nx
    last = cz - 1
    tile = 16

    def start(src, dst, i):
        copy = pltpu.make_async_copy(src, dst, sem.at[i])
        copy.start()
        return copy

    edges = [
        [
            start(p_ref.at[:, z], edge.at[e], 3 * e),
            start(u_ref.at[:, z], u_own.at[e], 3 * e + 1),
            start(k_ref.at[:, z], k_own.at[e], 3 * e + 2),
        ]
        for e, z in enumerate((0, last))
    ]
    inner = pl.ds(nx, cells - 2 * nx)
    load = start(turned_ref.at[inner], scr.at[inner], 6)
    stores = []
    for e, (z, un_ref, kn_ref) in enumerate(((0, ulo_ref, klo_ref), (last, uhi_ref, khi_ref))):
        for copy in edges[e]:
            copy.wait()

        def fix(t, carry):
            x = pl.multiple_of(t * tile, tile)
            for m in range(0, members, 8):
                at = (pl.ds(m, 8), pl.ds(x, tile), slice(None))
                u = u_own[(e,) + at].astype(jnp.float32)
                k = k_own[(e,) + at].astype(jnp.float32)
                un = un_ref[at].astype(jnp.float32)
                kn = kn_ref[at].astype(jnp.float32)
                new = edge[(e,) + at] + half_step * (k + kn) * (un - u)
                edge[(e,) + at] = new
                for i in range(0, tile, 8):
                    turned = jnp.swapaxes(new[:, i : i + 8, :], 0, 1)
                    scr[pl.ds(z * nx + x + i, 8), m : m + 8, :] = turned
            return carry

        lax.fori_loop(0, nx // tile, fix, 0)
        stores.append(start(edge.at[e], o_ref.at[:, z], 7 + e))
    load.wait()
    lane = lax.broadcasted_iota(jnp.int32, (members, ny), 1)
    unroll = 32

    def chunk(c, carry):
        def step(s, acc):
            for i in range(unroll):
                jj = s * unroll + i
                j = c * ny + jj
                v = pltpu.roll(scr[row_ref[j]], col_ref[j], 1)
                acc = jnp.where(lane == jj, v, acc)
            return acc

        acc = lax.fori_loop(0, ny // unroll, step, jnp.zeros((members, ny), jnp.float32))
        picked_ref[:, pl.ds(pl.multiple_of(c * ny, ny), ny)] = acc
        return carry

    lax.fori_loop(0, picked_ref.shape[1] // ny, chunk, 0)
    for copy in stores:
        copy.wait()


def border(pred, turned, u, k, ulo, klo, uhi, khi, position):
    m, cz, nx, ny = u.shape
    slots = position.shape[0]
    row = position // ny
    slot = jnp.arange(slots, dtype=jnp.int32)
    shift = (slot - position % ny) % ny
    smem = pl.BlockSpec(memory_space=pltpu.SMEM)
    vmem = pl.BlockSpec(memory_space=pltpu.VMEM)
    whole = pl.BlockSpec(memory_space=pl.ANY)
    return pl.pallas_call(
        border_kernel,
        in_specs=[smem, smem] + [whole] * 4 + [vmem] * 4,
        out_specs=[whole, vmem],
        out_shape=[
            jax.ShapeDtypeStruct(u.shape, jnp.float32),
            jax.ShapeDtypeStruct((m, slots), jnp.float32),
        ],
        scratch_shapes=[
            pltpu.VMEM(turned.shape, jnp.float32),
            pltpu.VMEM((2, m, nx, ny), jnp.float32),
            pltpu.VMEM((2, m, nx, ny), u.dtype),
            pltpu.VMEM((2, m, nx, ny), u.dtype),
            pltpu.SemaphoreType.DMA((9,)),
        ],
        input_output_aliases={2: 0},
        name="border",
    )(row, shift, pred, u, k, turned, ulo, klo, uhi, khi)


def products_kernel(
    n_e, n_s, count_ref, picked_ref, noise_ref, values_ref, std_ref, params_ref,
    gram_ref, cross_ref, all_params_ref,
    all_picked, part, paired, parts, total,
    send_a, recv_a, send_h, recv_h, send_p, recv_p, send_s, recv_s, send_g, recv_g,
):
    own, slots = picked_ref.shape
    members = own * n_e
    me_e, me_s = lax.axis_index("ens"), lax.axis_index("space")
    scale = math.sqrt(members - 1.0)

    def ens_peer(d):
        return (lax.rem(me_e + d, n_e), me_s)

    def space_peer(d):
        return (me_e, lax.rem(me_s + d, n_s))

    barrier = pltpu.get_barrier_semaphore()
    for d in range(1, n_e):
        pl.semaphore_signal(barrier, inc=1, device_id=ens_peer(d), device_id_type=MESH)
    space_pair = (me_e, me_s + 1 - 2 * lax.rem(me_s, 2))
    pl.semaphore_signal(barrier, inc=1, device_id=space_pair, device_id_type=MESH)
    for d in range(1, n_s // 2):
        pl.semaphore_signal(barrier, inc=1, device_id=space_peer(2 * d), device_id_type=MESH)
    pl.semaphore_wait(barrier, n_e - 1 + n_s // 2)

    def send(src, dst, ssem, rsem, peer):
        copy = pltpu.make_async_remote_copy(
            src_ref=src, dst_ref=dst, send_sem=ssem, recv_sem=rsem,
            device_id=peer, device_id_type=MESH,
        )
        copy.start()
        return copy

    pair = me_e + 1 - 2 * lax.rem(me_e, 2)
    partner = (pair, me_s)
    hops = n_e // 2
    handed = [send(picked_ref, all_picked.at[me_e], send_h.at[0], recv_h.at[0], partner)]
    picked_copies = [
        send(picked_ref, all_picked.at[me_e], send_a.at[d], recv_a.at[d], ens_peer(2 * d))
        for d in range(1, hops)
    ]
    params_copies = [
        send(params_ref, all_params_ref.at[me_e], send_p.at[d], recv_p.at[d], ens_peer(d))
        for d in range(1, n_e)
    ]
    all_params_ref[me_e] = params_ref[...]
    mine = picked_ref[...]
    all_picked[me_e] = mine
    live = lax.broadcasted_iota(jnp.int32, (1, slots), 1) < count_ref[0]
    std = std_ref[...]
    inverse = jnp.where(live, 1.0 / (std * scale), 0.0)
    misfit = jnp.where(live, (values_ref[...] - mine) / std + noise_ref[...], 0.0)
    for d in range(1, hops):
        picked_copies[d - 1].wait()
        block = all_picked.at[lax.rem(me_e + n_e - 2 * d, n_e)]
        handed.append(send(block, block, send_h.at[d], recv_h.at[d], partner))
    for copy in handed:
        copy.wait()
    everyone = all_picked[...].reshape(members, slots)
    centre = jnp.sum(everyone, axis=0, keepdims=True) / members
    spread = (everyone - centre) * inverse
    left = jnp.concatenate([(mine - centre) * inverse, misfit], axis=0)
    part[...] = lax.dot_general(
        left, spread, (((1,), (1,)), ((), ())),
        precision=HI, preferred_element_type=jnp.float32,
    )
    send(part, parts.at[0], send_s.at[0], recv_s.at[0], space_pair).wait()
    acc = part[...] + parts[0]
    paired[...] = acc
    space_copies = [
        send(paired, parts.at[d], send_s.at[d], recv_s.at[d], space_peer(2 * d))
        for d in range(1, n_s // 2)
    ]
    for d in range(1, n_s // 2):
        space_copies[d - 1].wait()
        acc += parts[d]
    total[...] = acc[:own]
    gram_copies = [
        send(total, gram_ref.at[me_e], send_g.at[d], recv_g.at[d], ens_peer(d))
        for d in range(1, n_e)
    ]
    gram_ref[me_e] = acc[:own]
    cross_ref[...] = acc[own:]
    for copy in gram_copies:
        copy.wait()
    for copy in params_copies:
        copy.wait()


def products(n_e, n_s, count, picked, noise, values, std, params):
    own, slots = picked.shape
    vmem = pl.BlockSpec(memory_space=pltpu.VMEM)
    dma = pltpu.SemaphoreType.DMA
    return pl.pallas_call(
        functools.partial(products_kernel, n_e, n_s),
        in_specs=[pl.BlockSpec(memory_space=pltpu.SMEM)] + [vmem] * 5,
        out_specs=[vmem] * 3,
        out_shape=[
            jax.ShapeDtypeStruct((n_e, own, n_e * own), jnp.float32),
            jax.ShapeDtypeStruct((own, n_e * own), jnp.float32),
            jax.ShapeDtypeStruct((n_e,) + params.shape, jnp.float32),
        ],
        scratch_shapes=[
            pltpu.VMEM((n_e, own, slots), jnp.float32),
            pltpu.VMEM((2 * own, n_e * own), jnp.float32),
            pltpu.VMEM((2 * own, n_e * own), jnp.float32),
            pltpu.VMEM((n_s // 2, 2 * own, n_e * own), jnp.float32),
            pltpu.VMEM((own, n_e * own), jnp.float32),
        ]
        + [dma((n_e,))] * 6 + [dma((n_s,))] * 2 + [dma((n_e,))] * 2,
        compiler_params=pltpu.CompilerParams(collective_id=0, has_side_effects=True),
        name="products",
    )(count, picked, noise, values.reshape(1, -1), std.reshape(1, -1), params)


def update_kernel(gram_ref, cross_ref, all_params_ref, params_ref, o_ref, work):
    members = gram_ref.shape[1]
    own = cross_ref.shape[0]
    rows = lax.broadcasted_iota(jnp.int32, (members, members), 0)
    cols = lax.broadcasted_iota(jnp.int32, (members, members), 1)
    lane = lax.broadcasted_iota(jnp.int32, (1, members), 1)
    work[:members] = gram_ref[...] + jnp.where(rows == cols, 1.0, 0.0)
    work[members:] = cross_ref[...]

    pivots = 8
    segments = 4
    span = members // segments

    def step(lo, s, diagonal):
        first = lo + s * pivots
        t = work[lo:]
        here = [lane == first + i for i in range(pivots)]
        columns = [
            jnp.sum(jnp.where(here[i], t, 0.0), axis=1, keepdims=True) for i in range(pivots)
        ]
        rows = [work[pl.ds(first + i, 1), :] for i in range(pivots)]
        corner = [
            [jnp.sum(jnp.where(here[j], rows[i], 0.0), axis=1, keepdims=True) for j in range(pivots)]
            for i in range(pivots)
        ]
        for i in range(pivots):
            pivot = corner[i][i]
            diagonal = jnp.where(here[i], pivot, diagonal)
            inverse = 1.0 / pivot
            factor = jnp.where(here[i], 0.0, rows[i] * inverse)
            t = t - columns[i] * factor
            for j in range(i + 1, pivots):
                ratio = corner[i][j] * inverse
                columns[j] = columns[j] - columns[i] * ratio
                rows[j] = rows[j] - corner[j][i] * factor
                for l in range(i + 1, pivots):
                    corner[l][j] = corner[l][j] - corner[l][i] * ratio
        work[lo:] = t
        return diagonal

    diagonal = jnp.ones((1, members), jnp.float32)
    for part in range(segments):
        diagonal = lax.fori_loop(
            0, span // pivots, functools.partial(step, part * span), diagonal
        )
    weights = work[members:] / diagonal
    all_params = all_params_ref[...]
    centre = jnp.sum(all_params, axis=0, keepdims=True) / members
    anomaly = (all_params - centre) / math.sqrt(members - 1.0)
    o_ref[...] = params_ref[...] + jnp.dot(
        weights, anomaly, precision=HI, preferred_element_type=jnp.float32
    )


def update(gram, cross, all_params, params):
    members, own = gram.shape[2], cross.shape[0]
    return pl.pallas_call(
        update_kernel,
        out_shape=jax.ShapeDtypeStruct(params.shape, jnp.float32),
        scratch_shapes=[pltpu.VMEM((members + own, members), jnp.float32)],
        name="update",
    )(gram.reshape(members, members), cross, all_params.reshape(members, -1), params)


def shards(n_e, n_s, u, k, position, count, values, std, noise, params):
    up = [(i, i + 1) for i in range(n_s - 1)]
    down = [(i + 1, i) for i in range(n_s - 1)]
    ulo = lax.ppermute(u[:, -1], "space", up)
    klo = lax.ppermute(k[:, -1], "space", up)
    uhi = lax.ppermute(u[:, 0], "space", down)
    khi = lax.ppermute(k[:, 0], "space", down)
    pred, turned = stencil(u, k)
    pred, picked = border(pred, turned, u, k, ulo, klo, uhi, khi, position)
    gram, cross, all_params = products(n_e, n_s, count, picked, noise, values, std, params)
    return update(gram, cross, all_params, params), pred


def solution(mesh):
    in_specs = (
        P("ens", "space", None, None),
        P("ens", "space", None, None),
        P("space"),
        P("space"),
        P("space"),
        P("space"),
        P("ens", "space"),
        P("ens", "space"),
    )
    out_specs = (P("ens", "space"), P("ens", "space", None, None))
    body = functools.partial(shards, mesh.shape["ens"], mesh.shape["space"])
    return jax.shard_map(body, mesh=mesh, in_specs=in_specs, out_specs=out_specs, check_vma=False)
```
